32 devices in a mesh: slab: 4 (over x, core), space: 8 (over z, y).
Axes of the slice: x: 2, y: 2, z: 4, core: 2. Of those that a mesh axis runs over, the one named last changes fastest.
Arguments:
- right_side: bfloat16 [4, 128, 64, 128], P('slab', 'space'), may hold values from -6 to 6
- lower_tiles: bfloat16 [4, 128, 6, 128, 128], P('slab', 'space'), may hold values from -0.1875 to 0.1875
- middle_tiles: bfloat16 [4, 128, 6, 128, 128], P('slab', 'space')
- upper_tiles: bfloat16 [4, 128, 6, 128, 128], P('slab', 'space'), may hold values from -0.1875 to 0.1875
- columns: int32 [4, 128, 6], P('slab', 'space'), may hold values from 0 to 127, as said below
- counts: int32 [4, 128], P('slab', 'space'), may hold values from 2 to 6, as said below
Outputs:
- solution: bfloat16 [4, 128, 64, 128], P('slab', 'space')
The draws below stay inside these ranges and needn't reach their ends.
Inputs may be any that keep to these rules, and one draw needn't show every extreme that they name: Slot 0 of tile row i holds i itself; slot 1 lies exactly 16 tile rows away from i, to either side; every other slot lies within 16 tile rows of i. Slots at or past the row's count hold valid columns but are unused. `counts`: in each slab some tile row uses all 6 slots.
All inputs are finite; a program needn't handle non-finite values.
Results may differ from the reference program's by a relative error of at most 0.023.
Values may be sent and summed in bfloat16 or wider, within the bound.
A program may use at most 64 MiB of HBM per device.

```python
import math
import jax
import jax.numpy as jnp
from jax import lax

TB = 128
ROWS_DEV = 16
K = 6
RHS = 64
SLABS = 4
TILE_ROWS = 128


def draw_middle_tiles(key, part):
    full_shape = (SLABS, TILE_ROWS, K, TB, TB)
    normal_part = jax.random.normal(key, full_shape, jnp.float32)
    slot_index = lax.broadcasted_iota(jnp.int32, full_shape, 2)
    row_index = lax.broadcasted_iota(jnp.int32, full_shape, 3)
    col_index = lax.broadcasted_iota(jnp.int32, full_shape, 4)
    spread = jnp.where(slot_index == 0, 0.4 / math.sqrt(TB), 0.4 / math.sqrt((K - 1) * TB))
    identity = jnp.where((slot_index == 0) & (row_index == col_index), 1.0, 0.0)
    return (identity + spread * normal_part).astype(jnp.bfloat16)


def draw_columns(key, part):
    key_near = jax.random.fold_in(key, 11)
    key_side = jax.random.fold_in(key, 12)
    row_index = jnp.arange(TILE_ROWS, dtype=jnp.int32)[None, :, None]
    offsets = jax.random.randint(key_near, (SLABS, TILE_ROWS, K), -ROWS_DEV, ROWS_DEV + 1)
    direction = jax.random.randint(key_side, (SLABS, TILE_ROWS, 1), 0, 2) * 2 - 1
    far_offset = direction * ROWS_DEV
    candidate = row_index + far_offset
    far_offset = jnp.where((candidate < 0) | (candidate >= TILE_ROWS), -far_offset, far_offset)
    slot_index = jnp.arange(K, dtype=jnp.int32)[None, None, :]
    offset = jnp.where(slot_index == 0, 0, jnp.where(slot_index == 1, far_offset, offsets))
    return jnp.clip(row_index + offset, 0, TILE_ROWS - 1).astype(jnp.int32)


def draw_counts(key, part):
    key_count = jax.random.fold_in(key, 21)
    key_row = jax.random.fold_in(key, 22)
    drawn = jax.random.randint(key_count, (SLABS, TILE_ROWS), 2, K + 1)
    chosen_row = jax.random.randint(key_row, (SLABS, 1), 0, TILE_ROWS)
    row_index = jnp.arange(TILE_ROWS, dtype=jnp.int32)[None, :]
    return jnp.where(row_index == chosen_row, K, drawn).astype(jnp.int32)


def block_scale(stream_key, extent, split, low, top_value):
    gain = 1.0
    for dim, parts in split:
        heights = jax.random.uniform(jax.random.fold_in(jax.random.fold_in(stream_key, 6), dim), (parts,), jnp.float32, low / len(split), top_value / len(split))
        gain = gain * jnp.repeat(jnp.exp(heights), extent[dim] // parts).reshape((-1,) + (1,) * (len(extent) - 1 - dim))
    return gain


def bell_draw(stream_key, extent, scale, bound, cuts=(), kind=jnp.bfloat16):
    values = scale * jax.random.normal(stream_key, extent, jnp.float32)
    if cuts:
        values = values * block_scale(stream_key, extent, cuts, -0.22, 0.18)
    return jnp.clip(values, -bound, bound).astype(kind)


def setup_inputs(seed: int = 0) -> dict:
    key_of = jax.random.split(jax.random.key(seed), 7)
    right_side = bell_draw(key_of[0], (SLABS, TILE_ROWS, RHS, TB), 1.0, 6.0, ((0, 4), (1, 8)))
    lower_tiles = bell_draw(key_of[1], (SLABS, TILE_ROWS, K, TB, TB), (3 * K * TB // 2) ** -0.5, 0.1875, ((0, 4), (1, 8)))
    middle_tiles = draw_middle_tiles(jax.random.fold_in(key_of[6], 71), 0)
    upper_tiles = bell_draw(key_of[3], (SLABS, TILE_ROWS, K, TB, TB), (3 * K * TB // 2) ** -0.5, 0.1875, ((0, 4), (1, 8)))
    columns = draw_columns(jax.random.fold_in(key_of[6], 71), 0)
    counts = draw_counts(jax.random.fold_in(key_of[6], 71), 0)
    return {"right_side": right_side, "lower_tiles": lower_tiles, "middle_tiles": middle_tiles, "upper_tiles": upper_tiles, "columns": columns, "counts": counts}


def product(tile_set, columns, counts, vector):
    picked = jnp.take(vector, columns, axis=0)
    in_use = jnp.arange(columns.shape[1], dtype=jnp.int32)[None, :] < counts[:, None]
    picked = jnp.where(in_use[:, :, None, None], picked, jnp.zeros((), picked.dtype))
    return jnp.einsum('ikab,ikrb->ira', tile_set.astype(jnp.float32), picked.astype(jnp.float32))


def reference(right_side, lower_tiles, middle_tiles, upper_tiles, columns, counts):
    nothing = jnp.zeros(right_side.shape[1:], jnp.bfloat16)

    def forward(previous, slab_items):
        source, lower, middle, slab_columns, slab_counts = slab_items
        forcing = (source.astype(jnp.float32) - product(lower, slab_columns, slab_counts, previous)).astype(jnp.bfloat16)
        sweep = product(middle, slab_columns, slab_counts, forcing).astype(jnp.bfloat16)
        return sweep, sweep

    _, sweeps = lax.scan(forward, nothing, (right_side, lower_tiles, middle_tiles, columns, counts))

    def backward(following, slab_items):
        sweep, upper, middle, slab_columns, slab_counts = slab_items
        coupled = product(upper, slab_columns, slab_counts, following).astype(jnp.bfloat16)
        result = (sweep.astype(jnp.float32) - product(middle, slab_columns, slab_counts, coupled)).astype(jnp.bfloat16)
        return result, result

    _, solution = lax.scan(backward, nothing, (sweeps, upper_tiles, middle_tiles, columns, counts), reverse=True)
    return solution
```

```python
import functools

import jax
import jax.numpy as jnp
from jax import lax
from jax.experimental import pallas as pl
from jax.experimental.pallas import tpu as pltpu
from jax.sharding import PartitionSpec as P

MESH = pl.DeviceIdType.MESH
GROUPS = 8
LAG = 3
UNROLL = 16
WAVE = 4
HOLD = 0
PREVIOUS, FORCING, FOLLOWING, COUPLED = 0, 1, 2, 3
LOW, OWN, HIGH = 0, 1, 2


def kernel(
    slabs, spaces,
    columns, counts, right_side, lower_hbm, middle_hbm, upper_hbm,
    out_hbm,
    lower, middle, upper, source, sweep, result, picks,
    tile_sem, source_sem, out_sem, send_sem, recv_sem,
    *halo_buffers,
):
    slab = lax.axis_index("slab")
    space = lax.axis_index("space")
    slots, _, rows = columns.shape
    groups, _, width, nodes = source.shape
    halo = [halo_buffers[kind * groups:(kind + 1) * groups] for kind in range(4)]
    previous, forcing, following, coupled = halo
    zero_row = 3 * rows

    has_low = space > 0
    has_high = space < spaces - 1
    side_exists = {LOW: has_low, OWN: None, HIGH: has_high}
    side_step = {LOW: -1, OWN: 0, HIGH: 1}

    def when_all(conditions, body):
        conditions = [c for c in conditions if c is not None]
        if not conditions:
            body()
            return
        total = conditions[0]
        for c in conditions[1:]:
            total = jnp.logical_and(total, c)
        pl.when(total)(body)

    tile_copies = [
        pltpu.make_async_copy(src, dst, tile_sem.at[n])
        for n, (src, dst) in enumerate(((middle_hbm, middle), (lower_hbm, lower), (upper_hbm, upper)))
    ]

    def group_slice(g):
        return pl.ds(g * width, width)

    def own_part(buffer, g):
        return buffer[g].at[pl.ds(rows, rows)]

    def source_copy(g, first):
        target = own_part(forcing, g) if first else source.at[g]
        return pltpu.make_async_copy(right_side.at[:, group_slice(g), :], target, source_sem.at[g])

    @pl.when(slab == 0)
    def _():
        for g in range(groups):
            source_copy(g, True).start()

    @pl.when(slab > 0)
    def _():
        for g in range(groups):
            source_copy(g, False).start()

    for copy in tile_copies:
        copy.start()

    barrier = pltpu.get_barrier_semaphore()
    slab_conditions = {-1: slab > 0, 0: None, 1: slab < slabs - 1}
    expected = jnp.int32(0)
    for slab_step in (-1, 0, 1):
        for side in (LOW, OWN, HIGH):
            if slab_step == 0 and side == OWN:
                continue
            conditions = [c for c in (slab_conditions[slab_step], side_exists[side]) if c is not None]

            def greet(slab_step=slab_step, side=side):
                pl.semaphore_signal(
                    barrier, inc=1,
                    device_id={"slab": slab + slab_step, "space": space + side_step[side]},
                    device_id_type=MESH,
                )

            when_all(conditions, greet)
            one = jnp.int32(1)
            for c in conditions:
                one = one * c.astype(jnp.int32)
            expected = expected + one

    for buffer in halo_buffers:
        buffer[zero_row] = jnp.zeros((width, nodes), buffer.dtype)

    @pl.when(jnp.logical_not(has_low))
    def _():
        for buffer in halo_buffers:
            buffer[0:rows] = jnp.zeros((rows, width, nodes), buffer.dtype)

    @pl.when(jnp.logical_not(has_high))
    def _():
        for buffer in halo_buffers:
            buffer[2 * rows:3 * rows] = jnp.zeros((rows, width, nodes), buffer.dtype)

    first_row = space * rows - rows

    def fill_picks(i, carry):
        for k in range(slots):
            picks[i * slots + k] = jnp.where(k < counts[0, i], columns[k, 0, i] - first_row, zero_row)
        return carry

    lax.fori_loop(0, rows, fill_picks, 0)
    pl.semaphore_wait(barrier, expected)

    def send(kind, g, side, slab_step, src):
        place = 2 - side
        return pltpu.make_async_remote_copy(
            src_ref=src,
            dst_ref=halo[kind][g].at[pl.ds(place * rows, rows)],
            send_sem=send_sem.at[kind, g, side],
            recv_sem=recv_sem.at[kind, g, place],
            device_id={"slab": slab + slab_step, "space": space + side_step[side]},
            device_id_type=MESH,
        )

    def sides_of(kind):
        return (LOW, HIGH) if kind in (FORCING, COUPLED) else (LOW, HIGH, OWN)

    def source_of(kind, g):
        if kind == FORCING:
            return own_part(forcing, g), 0
        if kind == COUPLED:
            return own_part(coupled, g), 0
        if kind == PREVIOUS:
            return sweep.at[g], 1
        return result.at[g], -1

    def start_sends(kind, g):
        src, slab_step = source_of(kind, g)
        for side in sides_of(kind):
            when_all([side_exists[side]], lambda side=side: send(kind, g, side, slab_step, src).start())

    def wait_sends(kind, g):
        src, slab_step = source_of(kind, g)
        for side in sides_of(kind):
            when_all([side_exists[side]], lambda side=side: send(kind, g, side, slab_step, src).wait_send())

    def wait_receives(kind, g):
        src, _ = source_of(kind, g)
        step = {PREVIOUS: -1, FOLLOWING: 1}.get(kind, 0)
        for place in sides_of(kind):
            when_all(
                [side_exists[place]],
                lambda place=place: pltpu.make_async_remote_copy(
                    src_ref=src,
                    dst_ref=halo[kind][g].at[pl.ds(place * rows, rows)],
                    send_sem=send_sem.at[kind, g, place],
                    recv_sem=recv_sem.at[kind, g, place],
                    device_id={"slab": slab + step, "space": space + side_step[place]},
                    device_id_type=MESH,
                ).wait_recv(),
            )

    def product(tiles, buffer, g, finish):
        def row(i, carry):
            vector = jnp.concatenate([buffer[g][picks[i * slots + k]] for k in range(slots)], axis=1)
            matrix = jnp.concatenate([tiles[i, k] for k in range(slots)], axis=0)
            total = jnp.dot(vector, matrix, preferred_element_type=jnp.float32)
            finish(i, total)
            return carry

        lax.fori_loop(0, rows, row, 0, unroll=UNROLL)

    def turn_over(tiles):
        def row(i, carry):
            for k in range(slots):
                tiles[i, k] = tiles[i, k].T
            return carry

        lax.fori_loop(0, rows, row, 0, unroll=2)

    @pl.when(slab == 0)
    def _():
        for g in range(min(WAVE, groups)):
            source_copy(g, True).wait()
            start_sends(FORCING, g)
        tile_copies[0].wait()
        turn_over(middle)

    @pl.when(slab > 0)
    def _():
        for g in range(groups):
            source_copy(g, False).wait()
        for copy, tiles in zip(tile_copies, (middle, lower, upper)):
            copy.wait()
            turn_over(tiles)

    def forcing_task(g):
        @pl.when(slab > 0)
        def _():
            wait_receives(PREVIOUS, g)

            def finish(i, total):
                forcing[g][rows + i] = (source[g, i].astype(jnp.float32) - total).astype(jnp.bfloat16)

            product(lower, previous, g, finish)
            start_sends(FORCING, g)

    def sweep_task(g):
        wait_receives(FORCING, g)

        @pl.when(slab < slabs - 1)
        def _():
            def finish(i, total):
                sweep[g, i] = total.astype(jnp.bfloat16)

            product(middle, forcing, g, finish)
            start_sends(PREVIOUS, g)

        @pl.when(slab == slabs - 1)
        def _():
            def finish(i, total):
                result[g, i] = total.astype(jnp.bfloat16)

            product(middle, forcing, g, finish)
            if slabs > 1:
                start_sends(FOLLOWING, g)
            out_copy(g).start()

    def out_copy(g):
        return pltpu.make_async_copy(result.at[g], out_hbm.at[:, group_slice(g), :], out_sem.at[g])

    def coupled_task(g):
        wait_receives(FOLLOWING, g)

        def finish(i, total):
            coupled[g][rows + i] = total.astype(jnp.bfloat16)

        product(upper, following, g, finish)
        start_sends(COUPLED, g)

    def solution_task(g):
        wait_receives(COUPLED, g)

        def finish(i, total):
            result[g, i] = (sweep[g, i].astype(jnp.float32) - total).astype(jnp.bfloat16)

        product(middle, coupled, g, finish)

        @pl.when(slab > 0)
        def _():
            start_sends(FOLLOWING, g)

        out_copy(g).start()

    def interleaved(first, second, between=None):
        for start in range(0, groups, WAVE):
            size = min(WAVE, groups - start)
            if between is not None and start > 0:
                between(start, size)
            for g in range(size + LAG):
                if g < size:
                    first(start + g)
                if 0 <= g - LAG < size:
                    second(start + g - LAG)

    def next_wave(start, size):
        @pl.when(slab == 0)
        def _():
            if slabs > 1:
                wait_sends(PREVIOUS, start - WAVE + HOLD)
            for g in range(start, start + size):
                source_copy(g, True).wait()
                start_sends(FORCING, g)

    held = [start - WAVE + HOLD for start in range(WAVE, groups, WAVE)] if slabs > 1 else []
    interleaved(forcing_task, sweep_task, next_wave)

    @pl.when(slab == 0)
    def _():
        tile_copies[1].wait()
        tile_copies[2].wait()
        turn_over(upper)

    @pl.when(slab < slabs - 1)
    def _():
        interleaved(coupled_task, solution_task)

    for g in range(groups):
        wait_sends(FORCING, g)

        @pl.when(slab < slabs - 1)
        def _():
            wait_sends(COUPLED, g)

        if g in held:
            @pl.when(jnp.logical_and(slab > 0, slab < slabs - 1))
            def _():
                wait_sends(PREVIOUS, g)
        else:
            @pl.when(slab < slabs - 1)
            def _():
                wait_sends(PREVIOUS, g)

        @pl.when(slab > 0)
        def _():
            wait_sends(FOLLOWING, g)

        out_copy(g).wait()


def solution(mesh):
    slabs, spaces = mesh.shape["slab"], mesh.shape["space"]

    def shards(right_side, lower_tiles, middle_tiles, upper_tiles, columns, counts):
        _, rows, rhs, nodes = right_side.shape
        slots = columns.shape[2]
        groups = GROUPS
        width = rhs // groups
        tile_shape = lower_tiles.shape[1:]
        halo_shape = (3 * rows + 1, width, nodes)
        block_shape = (groups, rows, width, nodes)
        out = pl.pallas_call(
            functools.partial(kernel, slabs, spaces),
            out_shape=jax.ShapeDtypeStruct((rows, rhs, nodes), jnp.bfloat16),
            in_specs=[pl.BlockSpec(memory_space=pltpu.SMEM)] * 2 + [pl.BlockSpec(memory_space=pltpu.MemorySpace.HBM)] * 4,
            out_specs=pl.BlockSpec(memory_space=pltpu.MemorySpace.HBM),
            scratch_shapes=[pltpu.VMEM(tile_shape, jnp.bfloat16)] * 3
            + [pltpu.VMEM(block_shape, jnp.bfloat16)] * 3
            + [
                pltpu.SMEM((rows * slots,), jnp.int32),
                pltpu.SemaphoreType.DMA((3,)),
                pltpu.SemaphoreType.DMA((groups,)),
                pltpu.SemaphoreType.DMA((groups,)),
                pltpu.SemaphoreType.DMA((4, groups, 3)),
                pltpu.SemaphoreType.DMA((4, groups, 3)),
            ]
            + [pltpu.VMEM(halo_shape, jnp.bfloat16)] * (4 * groups),
            compiler_params=pltpu.CompilerParams(
                collective_id=0, has_side_effects=True, vmem_limit_bytes=60 << 20
            ),
        )(columns.transpose(2, 0, 1), counts, right_side[0], lower_tiles[0], middle_tiles[0], upper_tiles[0])
        return out[None]

    in_specs = (
        P("slab", "space", None, None),
        P("slab", "space", None, None, None),
        P("slab", "space", None, None, None),
        P("slab", "space", None, None, None),
        P("slab", "space", None),
        P("slab", "space"),
    )
    out_specs = P("slab", "space", None, None)
    return jax.shard_map(shards, mesh=mesh, in_specs=in_specs, out_specs=out_specs, check_vma=False)
```

```python
import functools

import jax
import jax.numpy as jnp
from jax import lax
from jax.experimental import pallas as pl
from jax.experimental.pallas import tpu as pltpu
from jax.sharding import PartitionSpec as P

MESH = pl.DeviceIdType.MESH
GROUPS = 8
LAG = 4
UNROLL = 16
WAVE = 4
CREDIT = ("F", 3)
PREVIOUS, FORCING, FOLLOWING, COUPLED = 0, 1, 2, 3
LOW, OWN, HIGH = 0, 1, 2


def kernel(
    slabs, spaces,
    columns, counts, right_side, lower_hbm, middle_hbm, upper_hbm,
    out,
    lower, middle, upper, source, sweep, result, picks,
    tile_sem, source_sem, credit_sem, send_sem, recv_sem,
    *halo_buffers,
):
    slab = lax.axis_index("slab")
    space = lax.axis_index("space")
    slots, _, rows = columns.shape
    groups, _, width, nodes = source.shape
    halo = [halo_buffers[kind * groups:(kind + 1) * groups] for kind in range(4)]
    previous, forcing, following, coupled = halo
    zero_row = 3 * rows

    has_low = space > 0
    has_high = space < spaces - 1
    side_exists = {LOW: has_low, OWN: None, HIGH: has_high}
    side_step = {LOW: -1, OWN: 0, HIGH: 1}

    def when_all(conditions, body):
        conditions = [c for c in conditions if c is not None]
        if not conditions:
            body()
            return
        total = conditions[0]
        for c in conditions[1:]:
            total = jnp.logical_and(total, c)
        pl.when(total)(body)

    tile_copies = [
        pltpu.make_async_copy(src, dst, tile_sem.at[n])
        for n, (src, dst) in enumerate(((middle_hbm, middle), (lower_hbm, lower), (upper_hbm, upper)))
    ]

    def group_slice(g):
        return pl.ds(g * width, width)

    def own_part(buffer, g):
        return buffer[g].at[pl.ds(rows, rows)]

    def source_copy(g, first):
        target = own_part(forcing, g) if first else source.at[g]
        return pltpu.make_async_copy(right_side.at[:, group_slice(g), :], target, source_sem.at[g])

    @pl.when(slab == 0)
    def _():
        for g in range(groups):
            source_copy(g, True).start()

    @pl.when(slab > 0)
    def _():
        for g in range(groups):
            source_copy(g, False).start()

    for copy in tile_copies:
        copy.start()

    barrier = pltpu.get_barrier_semaphore()
    slab_conditions = {-1: slab > 0, 0: None, 1: slab < slabs - 1}
    expected = jnp.int32(0)
    for slab_step in (-1, 0, 1):
        for side in (LOW, OWN, HIGH):
            if slab_step == 0 and side == OWN:
                continue
            conditions = [c for c in (slab_conditions[slab_step], side_exists[side]) if c is not None]

            def greet(slab_step=slab_step, side=side):
                pl.semaphore_signal(
                    barrier, inc=1,
                    device_id={"slab": slab + slab_step, "space": space + side_step[side]},
                    device_id_type=MESH,
                )

            when_all(conditions, greet)
            one = jnp.int32(1)
            for c in conditions:
                one = one * c.astype(jnp.int32)
            expected = expected + one

    for buffer in halo_buffers:
        buffer[zero_row] = jnp.zeros((width, nodes), buffer.dtype)

    @pl.when(jnp.logical_not(has_low))
    def _():
        for buffer in halo_buffers:
            buffer[0:rows] = jnp.zeros((rows, width, nodes), buffer.dtype)

    @pl.when(jnp.logical_not(has_high))
    def _():
        for buffer in halo_buffers:
            buffer[2 * rows:3 * rows] = jnp.zeros((rows, width, nodes), buffer.dtype)

    first_row = space * rows - rows

    def fill_picks(i, carry):
        for k in range(slots):
            picks[i * slots + k] = jnp.where(k < counts[0, i], columns[k, 0, i] - first_row, zero_row)
        return carry

    lax.fori_loop(0, rows, fill_picks, 0)
    pl.semaphore_wait(barrier, expected)

    def send(kind, g, side, slab_step, src):
        place = 2 - side
        return pltpu.make_async_remote_copy(
            src_ref=src,
            dst_ref=halo[kind][g].at[pl.ds(place * rows, rows)],
            send_sem=send_sem.at[kind, g, side],
            recv_sem=recv_sem.at[kind, g, place],
            device_id={"slab": slab + slab_step, "space": space + side_step[side]},
            device_id_type=MESH,
        )

    def sides_of(kind):
        return (LOW, HIGH) if kind in (FORCING, COUPLED) else (LOW, HIGH, OWN)

    def source_of(kind, g):
        if kind == FORCING:
            return own_part(forcing, g), 0
        if kind == COUPLED:
            return own_part(coupled, g), 0
        if kind == PREVIOUS:
            return sweep.at[g], 1
        return result.at[g], -1

    even = lax.rem(space, 2) == 0

    def start_sends(kind, g):
        src, slab_step = source_of(kind, g)
        for first, conditions in ((LOW, [even]), (HIGH, [jnp.logical_not(even)])):

            def both(first=first):
                for side in (first, LOW + HIGH - first):
                    when_all([side_exists[side]], lambda side=side: send(kind, g, side, slab_step, src).start())

            when_all(conditions, both)
        if OWN in sides_of(kind):
            send(kind, g, OWN, slab_step, src).start()

    def wait_sends(kind, g):
        src, slab_step = source_of(kind, g)
        for side in sides_of(kind):
            when_all([side_exists[side]], lambda side=side: send(kind, g, side, slab_step, src).wait_send())

    def wait_receives(kind, g):
        src, _ = source_of(kind, g)
        step = {PREVIOUS: -1, FOLLOWING: 1}.get(kind, 0)
        for place in sides_of(kind):
            when_all(
                [side_exists[place]],
                lambda place=place: pltpu.make_async_remote_copy(
                    src_ref=src,
                    dst_ref=halo[kind][g].at[pl.ds(place * rows, rows)],
                    send_sem=send_sem.at[kind, g, place],
                    recv_sem=recv_sem.at[kind, g, place],
                    device_id={"slab": slab + step, "space": space + side_step[place]},
                    device_id_type=MESH,
                ).wait_recv(),
            )

    def product(tiles, buffer, g, finish):
        def row(i, carry):
            vector = jnp.concatenate([buffer[g][picks[i * slots + k]] for k in range(slots)], axis=1)
            matrix = jnp.concatenate([tiles[i, k] for k in range(slots)], axis=0)
            total = jnp.dot(vector, matrix, preferred_element_type=jnp.float32)
            finish(i, total)
            return carry

        lax.fori_loop(0, rows, row, 0, unroll=UNROLL)

    def turn_over(tiles):
        def row(i, carry):
            for k in range(slots):
                tiles[i, k] = tiles[i, k].T
            return carry

        lax.fori_loop(0, rows, row, 0, unroll=2)

    @pl.when(slab == 0)
    def _():
        for g in range(min(WAVE, groups)):
            source_copy(g, True).wait()
            start_sends(FORCING, g)
        tile_copies[0].wait()
        turn_over(middle)

    @pl.when(slab > 0)
    def _():
        for g in range(groups):
            source_copy(g, False).wait()
        for copy, tiles in zip(tile_copies, (middle, lower, upper)):
            copy.wait()
            turn_over(tiles)

    def forcing_task(g):
        @pl.when(slab > 0)
        def _():
            wait_receives(PREVIOUS, g)

            def finish(i, total):
                forcing[g][rows + i] = (source[g, i].astype(jnp.float32) - total).astype(jnp.bfloat16)

            product(lower, previous, g, finish)
            start_sends(FORCING, g)

        give_credit("F", g)

    def sweep_task(g):
        wait_receives(FORCING, g)

        @pl.when(slab < slabs - 1)
        def _():
            def finish(i, total):
                sweep[g, i] = total.astype(jnp.bfloat16)

            product(middle, forcing, g, finish)
            start_sends(PREVIOUS, g)

        @pl.when(slab == slabs - 1)
        def _():
            def finish(i, total):
                value = total.astype(jnp.bfloat16)
                result[g, i] = value
                out[i, group_slice(g), :] = value

            product(middle, forcing, g, finish)
            if slabs > 1:
                start_sends(FOLLOWING, g)

        give_credit("S", g)

    def coupled_task(g):
        wait_receives(FOLLOWING, g)

        def finish(i, total):
            coupled[g][rows + i] = total.astype(jnp.bfloat16)

        product(upper, following, g, finish)
        start_sends(COUPLED, g)

    def solution_task(g):
        wait_receives(COUPLED, g)

        def finish(i, total):
            value = (sweep[g, i].astype(jnp.float32) - total).astype(jnp.bfloat16)
            result[g, i] = value
            out[i, group_slice(g), :] = value

        product(middle, coupled, g, finish)

        @pl.when(slab > 0)
        def _():
            start_sends(FOLLOWING, g)

    def interleaved(first, second, between=None):
        for start in range(0, groups, WAVE):
            size = min(WAVE, groups - start)
            if between is not None and start > 0:
                between(start, size)
            for g in range(size + LAG):
                if g < size:
                    first(start + g)
                if 0 <= g - LAG < size:
                    second(start + g - LAG)

    def next_wave(start, size):
        @pl.when(slab == 0)
        def _():
            if slabs > 1:
                pl.semaphore_wait(credit_sem, 1)
            for g in range(start, start + size):
                source_copy(g, True).wait()
                start_sends(FORCING, g)

    def give_credit(name, g):
        if CREDIT[0] == name and (g - CREDIT[1]) % WAVE == 0 and g - CREDIT[1] + WAVE < groups:
            @pl.when(slab == 1)
            def _():
                pl.semaphore_signal(
                    credit_sem, inc=1, device_id={"slab": slab - 1, "space": space}, device_id_type=MESH
                )

    interleaved(forcing_task, sweep_task, next_wave)

    @pl.when(slab == 0)
    def _():
        tile_copies[1].wait()
        tile_copies[2].wait()
        turn_over(upper)

    @pl.when(slab < slabs - 1)
    def _():
        interleaved(coupled_task, solution_task)

    for g in range(groups):
        wait_sends(FORCING, g)

        @pl.when(slab < slabs - 1)
        def _():
            wait_sends(PREVIOUS, g)
            wait_sends(COUPLED, g)

        @pl.when(slab > 0)
        def _():
            wait_sends(FOLLOWING, g)


def solution(mesh):
    slabs, spaces = mesh.shape["slab"], mesh.shape["space"]

    def shards(right_side, lower_tiles, middle_tiles, upper_tiles, columns, counts):
        _, rows, rhs, nodes = right_side.shape
        slots = columns.shape[2]
        groups = GROUPS
        width = rhs // groups
        tile_shape = lower_tiles.shape[1:]
        halo_shape = (3 * rows + 1, width, nodes)
        block_shape = (groups, rows, width, nodes)
        out = pl.pallas_call(
            functools.partial(kernel, slabs, spaces),
            out_shape=pltpu.VMEM((rows, rhs, nodes), jnp.bfloat16),
            in_specs=[pl.BlockSpec(memory_space=pltpu.SMEM)] * 2 + [pl.BlockSpec(memory_space=pltpu.MemorySpace.HBM)] * 4,
            out_specs=pl.BlockSpec(memory_space=pltpu.VMEM),
            scratch_shapes=[pltpu.VMEM(tile_shape, jnp.bfloat16)] * 3
            + [pltpu.VMEM(block_shape, jnp.bfloat16)] * 3
            + [
                pltpu.SMEM((rows * slots,), jnp.int32),
                pltpu.SemaphoreType.DMA((3,)),
                pltpu.SemaphoreType.DMA((groups,)),
                pltpu.SemaphoreType.REGULAR,
                pltpu.SemaphoreType.DMA((4, groups, 3)),
                pltpu.SemaphoreType.DMA((4, groups, 3)),
            ]
            + [pltpu.VMEM(halo_shape, jnp.bfloat16)] * (4 * groups),
            compiler_params=pltpu.CompilerParams(
                collective_id=0, has_side_effects=True, vmem_limit_bytes=60 << 20
            ),
        )(columns.transpose(2, 0, 1), counts, right_side[0], lower_tiles[0], middle_tiles[0], upper_tiles[0])
        return out[None]

    in_specs = (
        P("slab", "space", None, None),
        P("slab", "space", None, None, None),
        P("slab", "space", None, None, None),
        P("slab", "space", None, None, None),
        P("slab", "space", None),
        P("slab", "space"),
    )
    out_specs = P("slab", "space", None, None)
    return jax.shard_map(shards, mesh=mesh, in_specs=in_specs, out_specs=out_specs, check_vma=False)
```

```python
import functools

import jax
import jax.numpy as jnp
from jax import lax
from jax.experimental import pallas as pl
from jax.experimental.pallas import tpu as pltpu
from jax.sharding import PartitionSpec as P

MESH = pl.DeviceIdType.MESH
GROUPS = 8
LAG = 4
UNROLL = 16
WAVE = 4
CREDIT = ("F", 3)
PREVIOUS, FORCING, FOLLOWING, COUPLED = 0, 1, 2, 3
LOW, OWN, HIGH = 0, 1, 2


def kernel(
    slabs, spaces,
    columns, counts, right_side, lower_hbm, middle_hbm, upper_hbm,
    out,
    lower, middle, upper, source, sweep, result, picks,
    tile_sem, source_sem, credit_sem, send_sem, recv_sem,
    *halo_buffers,
):
    slab = lax.axis_index("slab")
    space = lax.axis_index("space")
    slots, _, rows = columns.shape
    groups, _, width, nodes = source.shape
    halo = [halo_buffers[kind * groups:(kind + 1) * groups] for kind in range(4)]
    previous, forcing, following, coupled = halo
    zero_row = 3 * rows

    has_low = space > 0
    has_high = space < spaces - 1
    side_exists = {LOW: has_low, OWN: None, HIGH: has_high}
    side_step = {LOW: -1, OWN: 0, HIGH: 1}

    def when_all(conditions, body):
        conditions = [c for c in conditions if c is not None]
        if not conditions:
            body()
            return
        total = conditions[0]
        for c in conditions[1:]:
            total = jnp.logical_and(total, c)
        pl.when(total)(body)

    tile_copies = [
        pltpu.make_async_copy(src, dst, tile_sem.at[n])
        for n, (src, dst) in enumerate(((middle_hbm, middle), (lower_hbm, lower), (upper_hbm, upper)))
    ]

    def group_slice(g):
        return pl.ds(g * width, width)

    def own_part(buffer, g):
        return buffer[g].at[pl.ds(rows, rows)]

    def source_copy(g, first):
        target = own_part(forcing, g) if first else source.at[g]
        return pltpu.make_async_copy(right_side.at[:, group_slice(g), :], target, source_sem.at[g])

    @pl.when(slab == 0)
    def _():
        for g in range(groups):
            source_copy(g, True).start()

    @pl.when(slab > 0)
    def _():
        for g in range(groups):
            source_copy(g, False).start()

    for copy in tile_copies:
        copy.start()

    barrier = pltpu.get_barrier_semaphore()
    slab_conditions = {-1: slab > 0, 0: None, 1: slab < slabs - 1}
    expected = jnp.int32(0)
    for slab_step in (-1, 0, 1):
        for side in (LOW, OWN, HIGH):
            if slab_step == 0 and side == OWN:
                continue
            conditions = [c for c in (slab_conditions[slab_step], side_exists[side]) if c is not None]

            def greet(slab_step=slab_step, side=side):
                pl.semaphore_signal(
                    barrier, inc=1,
                    device_id={"slab": slab + slab_step, "space": space + side_step[side]},
                    device_id_type=MESH,
                )

            when_all(conditions, greet)
            one = jnp.int32(1)
            for c in conditions:
                one = one * c.astype(jnp.int32)
            expected = expected + one

    for buffer in halo_buffers:
        buffer[zero_row] = jnp.zeros((width, nodes), buffer.dtype)

    @pl.when(jnp.logical_not(has_low))
    def _():
        for buffer in halo_buffers:
            buffer[0:rows] = jnp.zeros((rows, width, nodes), buffer.dtype)

    @pl.when(jnp.logical_not(has_high))
    def _():
        for buffer in halo_buffers:
            buffer[2 * rows:3 * rows] = jnp.zeros((rows, width, nodes), buffer.dtype)

    first_row = space * rows - rows

    def fill_picks(i, carry):
        for k in range(slots):
            picks[i * slots + k] = jnp.where(k < counts[0, i], columns[k, 0, i] - first_row, zero_row)
        return carry

    lax.fori_loop(0, rows, fill_picks, 0)
    pl.semaphore_wait(barrier, expected)

    def send(kind, g, side, slab_step, src):
        place = 2 - side
        return pltpu.make_async_remote_copy(
            src_ref=src,
            dst_ref=halo[kind][g].at[pl.ds(place * rows, rows)],
            send_sem=send_sem.at[kind, g, side],
            recv_sem=recv_sem.at[kind, g, place],
            device_id={"slab": slab + slab_step, "space": space + side_step[side]},
            device_id_type=MESH,
        )

    def sides_of(kind):
        return (LOW, HIGH) if kind in (FORCING, COUPLED) else (LOW, HIGH, OWN)

    def source_of(kind, g):
        if kind == FORCING:
            return own_part(forcing, g), 0
        if kind == COUPLED:
            return own_part(coupled, g), 0
        if kind == PREVIOUS:
            return sweep.at[g], 1
        return result.at[g], -1

    even = lax.rem(space, 2) == 0

    def start_sends(kind, g):
        src, slab_step = source_of(kind, g)
        for first, conditions in ((LOW, [even]), (HIGH, [jnp.logical_not(even)])):

            def both(first=first):
                for side in (first, LOW + HIGH - first):
                    when_all([side_exists[side]], lambda side=side: send(kind, g, side, slab_step, src).start())

            when_all(conditions, both)
        if OWN in sides_of(kind):
            send(kind, g, OWN, slab_step, src).start()

    def wait_sends(kind, g):
        src, slab_step = source_of(kind, g)
        for side in sides_of(kind):
            when_all([side_exists[side]], lambda side=side: send(kind, g, side, slab_step, src).wait_send())

    def wait_receives(kind, g):
        src, _ = source_of(kind, g)
        step = {PREVIOUS: -1, FOLLOWING: 1}.get(kind, 0)
        for place in sides_of(kind):
            when_all(
                [side_exists[place]],
                lambda place=place: pltpu.make_async_remote_copy(
                    src_ref=src,
                    dst_ref=halo[kind][g].at[pl.ds(place * rows, rows)],
                    send_sem=send_sem.at[kind, g, place],
                    recv_sem=recv_sem.at[kind, g, place],
                    device_id={"slab": slab + step, "space": space + side_step[place]},
                    device_id_type=MESH,
                ).wait_recv(),
            )

    def product(tiles, buffer, g, finish):
        def row(i, carry):
            vector = jnp.concatenate([buffer[g][picks[i * slots + k]] for k in range(slots)], axis=1)
            matrix = jnp.concatenate([tiles[i, k] for k in range(slots)], axis=0)
            total = jnp.dot(vector, matrix, preferred_element_type=jnp.float32)
            finish(i, total)
            return carry

        lax.fori_loop(0, rows, row, 0, unroll=UNROLL)

    def turn_over(tiles):
        def row(i, carry):
            for k in range(slots):
                tiles[i, k] = tiles[i, k].T
            return carry

        lax.fori_loop(0, rows, row, 0, unroll=2)

    @pl.when(slab == 0)
    def _():
        for g in range(min(WAVE, groups)):
            source_copy(g, True).wait()
            start_sends(FORCING, g)
        tile_copies[0].wait()
        turn_over(middle)

    @pl.when(slab > 0)
    def _():
        for g in range(groups):
            source_copy(g, False).wait()
        for copy, tiles in zip(tile_copies, (middle, lower, upper)):
            copy.wait()
            turn_over(tiles)

    def forcing_task(g):
        @pl.when(slab > 0)
        def _():
            wait_receives(PREVIOUS, g)

            def finish(i, total):
                forcing[g][rows + i] = (source[g, i].astype(jnp.float32) - total).astype(jnp.bfloat16)

            product(lower, previous, g, finish)
            start_sends(FORCING, g)

        give_credit("F", g)

    def sweep_task(g):
        wait_receives(FORCING, g)

        @pl.when(slab < slabs - 1)
        def _():
            def finish(i, total):
                sweep[g, i] = total.astype(jnp.bfloat16)

            product(middle, forcing, g, finish)
            start_sends(PREVIOUS, g)

        @pl.when(slab == slabs - 1)
        def _():
            def finish(i, total):
                value = total.astype(jnp.bfloat16)
                result[g, i] = value
                out[i, group_slice(g), :] = value

            product(middle, forcing, g, finish)
            if slabs > 1:
                start_sends(FOLLOWING, g)

        give_credit("S", g)

    def coupled_task(g):
        wait_receives(FOLLOWING, g)

        def finish(i, total):
            coupled[g][rows + i] = total.astype(jnp.bfloat16)

        product(upper, following, g, finish)
        start_sends(COUPLED, g)

    def solution_task(g):
        wait_receives(COUPLED, g)

        def finish(i, total):
            value = (sweep[g, i].astype(jnp.float32) - total).astype(jnp.bfloat16)
            result[g, i] = value
            out[i, group_slice(g), :] = value

        product(middle, coupled, g, finish)

        @pl.when(slab > 0)
        def _():
            start_sends(FOLLOWING, g)

    def interleaved(first, second, between=None, after=None):
        for start in range(0, groups, WAVE):
            size = min(WAVE, groups - start)
            if between is not None and start > 0:
                between(start, size)
            for g in range(size + LAG):
                if g < size:
                    first(start + g)
                if 0 <= g - LAG < size:
                    second(start + g - LAG)
            if after is not None and start + size < groups:
                after(start, size)

    def next_wave(start, size):
        @pl.when(slab == 0)
        def _():
            if slabs > 1:
                pl.semaphore_wait(credit_sem, 1)
            for g in range(start, start + size):
                source_copy(g, True).wait()
                start_sends(FORCING, g)

    def give_credit(name, g):
        if CREDIT[0] == name and (g - CREDIT[1]) % WAVE == 0 and g - CREDIT[1] + WAVE < groups:
            @pl.when(slab == 1)
            def _():
                pl.semaphore_signal(
                    credit_sem, inc=1, device_id={"slab": slab - 1, "space": space}, device_id_type=MESH
                )

    interleaved(forcing_task, sweep_task, next_wave)

    @pl.when(slab == 0)
    def _():
        tile_copies[1].wait()
        tile_copies[2].wait()
        turn_over(upper)
        for g in range(groups):
            wait_sends(FORCING, g)
            if slabs > 1:
                wait_sends(PREVIOUS, g)

    def wave_sent(start, size):
        for g in range(start, start + size):
            wait_sends(COUPLED, g)

    @pl.when(slab < slabs - 1)
    def _():
        interleaved(coupled_task, solution_task, after=wave_sent)

    last_wave = groups - WAVE

    @pl.when(slab > 0)
    def _():
        for g in range(groups):
            wait_sends(FORCING, g)
            wait_sends(FOLLOWING, g)

            @pl.when(slab < slabs - 1)
            def _():
                wait_sends(PREVIOUS, g)

    if slabs > 1:

        @pl.when(slab < slabs - 1)
        def _():
            for g in range(last_wave, groups):
                wait_sends(COUPLED, g)


def solution(mesh):
    slabs, spaces = mesh.shape["slab"], mesh.shape["space"]

    def shards(right_side, lower_tiles, middle_tiles, upper_tiles, columns, counts):
        _, rows, rhs, nodes = right_side.shape
        slots = columns.shape[2]
        groups = GROUPS
        width = rhs // groups
        tile_shape = lower_tiles.shape[1:]
        halo_shape = (3 * rows + 1, width, nodes)
        block_shape = (groups, rows, width, nodes)
        out = pl.pallas_call(
            functools.partial(kernel, slabs, spaces),
            out_shape=pltpu.VMEM((rows, rhs, nodes), jnp.bfloat16),
            in_specs=[pl.BlockSpec(memory_space=pltpu.SMEM)] * 2 + [pl.BlockSpec(memory_space=pltpu.MemorySpace.HBM)] * 4,
            out_specs=pl.BlockSpec(memory_space=pltpu.VMEM),
            scratch_shapes=[pltpu.VMEM(tile_shape, jnp.bfloat16)] * 3
            + [pltpu.VMEM(block_shape, jnp.bfloat16)] * 3
            + [
                pltpu.SMEM((rows * slots,), jnp.int32),
                pltpu.SemaphoreType.DMA((3,)),
                pltpu.SemaphoreType.DMA((groups,)),
                pltpu.SemaphoreType.REGULAR,
                pltpu.SemaphoreType.DMA((4, groups, 3)),
                pltpu.SemaphoreType.DMA((4, groups, 3)),
            ]
            + [pltpu.VMEM(halo_shape, jnp.bfloat16)] * (4 * groups),
            compiler_params=pltpu.CompilerParams(
                collective_id=0, has_side_effects=True, vmem_limit_bytes=60 << 20
            ),
        )(columns.transpose(2, 0, 1), counts, right_side[0], lower_tiles[0], middle_tiles[0], upper_tiles[0])
        return out[None]

    in_specs = (
        P("slab", "space", None, None),
        P("slab", "space", None, None, None),
        P("slab", "space", None, None, None),
        P("slab", "space", None, None, None),
        P("slab", "space", None),
        P("slab", "space"),
    )
    out_specs = P("slab", "space", None, None)
    return jax.shard_map(shards, mesh=mesh, in_specs=in_specs, out_specs=out_specs, check_vma=False)
```

```python
import functools

import jax
import jax.numpy as jnp
from jax import lax
from jax.experimental import pallas as pl
from jax.experimental.pallas import tpu as pltpu
from jax.sharding import PartitionSpec as P

MESH = pl.DeviceIdType.MESH
GROUPS = 8
LAG = 4
LAG_BACK = 3
UNROLL = 16
WAVE = 4
CREDIT = ("F", 3)
PREVIOUS, FORCING, FOLLOWING, COUPLED = 0, 1, 2, 3
LOW, OWN, HIGH = 0, 1, 2


def kernel(
    slabs, spaces,
    columns, counts, right_side, lower_hbm, middle_hbm, upper_hbm,
    out,
    lower, middle, upper, source, sweep, result, picks,
    tile_sem, source_sem, credit_sem, send_sem, recv_sem,
    *halo_buffers,
):
    slab = lax.axis_index("slab")
    space = lax.axis_index("space")
    slots, _, rows = columns.shape
    groups, _, width, nodes = source.shape
    halo = [halo_buffers[kind * groups:(kind + 1) * groups] for kind in range(4)]
    previous, forcing, following, coupled = halo
    zero_row = 3 * rows

    has_low = space > 0
    has_high = space < spaces - 1
    side_exists = {LOW: has_low, OWN: None, HIGH: has_high}
    side_step = {LOW: -1, OWN: 0, HIGH: 1}

    def when_all(conditions, body):
        conditions = [c for c in conditions if c is not None]
        if not conditions:
            body()
            return
        total = conditions[0]
        for c in conditions[1:]:
            total = jnp.logical_and(total, c)
        pl.when(total)(body)

    tile_copies = [
        pltpu.make_async_copy(src, dst, tile_sem.at[n])
        for n, (src, dst) in enumerate(((middle_hbm, middle), (lower_hbm, lower), (upper_hbm, upper)))
    ]

    def group_slice(g):
        return pl.ds(g * width, width)

    def own_part(buffer, g):
        return buffer[g].at[pl.ds(rows, rows)]

    def source_copy(g, first):
        target = own_part(forcing, g) if first else source.at[g]
        return pltpu.make_async_copy(right_side.at[:, group_slice(g), :], target, source_sem.at[g])

    @pl.when(slab == 0)
    def _():
        for g in range(groups):
            source_copy(g, True).start()

    @pl.when(slab > 0)
    def _():
        for g in range(groups):
            source_copy(g, False).start()

    for copy in tile_copies:
        copy.start()

    barrier = pltpu.get_barrier_semaphore()
    slab_conditions = {-1: slab > 0, 0: None, 1: slab < slabs - 1}
    expected = jnp.int32(0)
    for slab_step in (-1, 0, 1):
        for side in (LOW, OWN, HIGH):
            if slab_step == 0 and side == OWN:
                continue
            conditions = [c for c in (slab_conditions[slab_step], side_exists[side]) if c is not None]

            def greet(slab_step=slab_step, side=side):
                pl.semaphore_signal(
                    barrier, inc=1,
                    device_id={"slab": slab + slab_step, "space": space + side_step[side]},
                    device_id_type=MESH,
                )

            when_all(conditions, greet)
            one = jnp.int32(1)
            for c in conditions:
                one = one * c.astype(jnp.int32)
            expected = expected + one

    for buffer in halo_buffers:
        buffer[zero_row] = jnp.zeros((width, nodes), buffer.dtype)

    @pl.when(jnp.logical_not(has_low))
    def _():
        for buffer in halo_buffers:
            buffer[0:rows] = jnp.zeros((rows, width, nodes), buffer.dtype)

    @pl.when(jnp.logical_not(has_high))
    def _():
        for buffer in halo_buffers:
            buffer[2 * rows:3 * rows] = jnp.zeros((rows, width, nodes), buffer.dtype)

    first_row = space * rows - rows

    def fill_picks(i, carry):
        for k in range(slots):
            picks[i * slots + k] = jnp.where(k < counts[0, i], columns[k, 0, i] - first_row, zero_row)
        return carry

    lax.fori_loop(0, rows, fill_picks, 0)
    pl.semaphore_wait(barrier, expected)

    def send(kind, g, side, slab_step, src):
        place = 2 - side
        return pltpu.make_async_remote_copy(
            src_ref=src,
            dst_ref=halo[kind][g].at[pl.ds(place * rows, rows)],
            send_sem=send_sem.at[kind, g, side],
            recv_sem=recv_sem.at[kind, g, place],
            device_id={"slab": slab + slab_step, "space": space + side_step[side]},
            device_id_type=MESH,
        )

    def sides_of(kind):
        return (LOW, HIGH) if kind in (FORCING, COUPLED) else (LOW, HIGH, OWN)

    def source_of(kind, g):
        if kind == FORCING:
            return own_part(forcing, g), 0
        if kind == COUPLED:
            return own_part(coupled, g), 0
        if kind == PREVIOUS:
            return sweep.at[g], 1
        return result.at[g], -1

    even = lax.rem(space, 2) == 0

    def start_sends(kind, g):
        src, slab_step = source_of(kind, g)
        for first, conditions in ((LOW, [even]), (HIGH, [jnp.logical_not(even)])):

            def both(first=first):
                for side in (first, LOW + HIGH - first):
                    when_all([side_exists[side]], lambda side=side: send(kind, g, side, slab_step, src).start())

            when_all(conditions, both)
        if OWN in sides_of(kind):
            send(kind, g, OWN, slab_step, src).start()

    def wait_sends(kind, g):
        src, slab_step = source_of(kind, g)
        for side in sides_of(kind):
            when_all([side_exists[side]], lambda side=side: send(kind, g, side, slab_step, src).wait_send())

    def wait_receives(kind, g):
        src, _ = source_of(kind, g)
        step = {PREVIOUS: -1, FOLLOWING: 1}.get(kind, 0)
        for place in sides_of(kind):
            when_all(
                [side_exists[place]],
                lambda place=place: pltpu.make_async_remote_copy(
                    src_ref=src,
                    dst_ref=halo[kind][g].at[pl.ds(place * rows, rows)],
                    send_sem=send_sem.at[kind, g, place],
                    recv_sem=recv_sem.at[kind, g, place],
                    device_id={"slab": slab + step, "space": space + side_step[place]},
                    device_id_type=MESH,
                ).wait_recv(),
            )

    def product(tiles, buffer, g, finish):
        def row(i, carry):
            vector = jnp.concatenate([buffer[g][picks[i * slots + k]] for k in range(slots)], axis=1)
            matrix = jnp.concatenate([tiles[i, k] for k in range(slots)], axis=0)
            total = jnp.dot(vector, matrix, preferred_element_type=jnp.float32)
            finish(i, total)
            return carry

        lax.fori_loop(0, rows, row, 0, unroll=UNROLL)

    def turn_over(tiles):
        def row(i, carry):
            for k in range(slots):
                tiles[i, k] = tiles[i, k].T
            return carry

        lax.fori_loop(0, rows, row, 0, unroll=8)

    @pl.when(slab == 0)
    def _():
        for g in range(min(WAVE, groups)):
            source_copy(g, True).wait()
            start_sends(FORCING, g)
        tile_copies[0].wait()
        turn_over(middle)

    @pl.when(slab > 0)
    def _():
        for g in range(groups):
            source_copy(g, False).wait()
        for copy, tiles in zip(tile_copies, (middle, lower, upper)):
            copy.wait()
            turn_over(tiles)

    def forcing_task(g):
        @pl.when(slab > 0)
        def _():
            wait_receives(PREVIOUS, g)

            def finish(i, total):
                forcing[g][rows + i] = (source[g, i].astype(jnp.float32) - total).astype(jnp.bfloat16)

            product(lower, previous, g, finish)
            start_sends(FORCING, g)

        give_credit("F", g)

    def sweep_task(g):
        wait_receives(FORCING, g)

        @pl.when(slab < slabs - 1)
        def _():
            def finish(i, total):
                sweep[g, i] = total.astype(jnp.bfloat16)

            product(middle, forcing, g, finish)
            start_sends(PREVIOUS, g)

        @pl.when(slab == slabs - 1)
        def _():
            def finish(i, total):
                value = total.astype(jnp.bfloat16)
                result[g, i] = value
                out[i, group_slice(g), :] = value

            product(middle, forcing, g, finish)
            if slabs > 1:
                start_sends(FOLLOWING, g)

        give_credit("S", g)

    def coupled_task(g):
        wait_receives(FOLLOWING, g)

        def finish(i, total):
            coupled[g][rows + i] = total.astype(jnp.bfloat16)

        product(upper, following, g, finish)
        start_sends(COUPLED, g)

    def solution_task(g):
        wait_receives(COUPLED, g)

        def finish(i, total):
            value = (sweep[g, i].astype(jnp.float32) - total).astype(jnp.bfloat16)
            result[g, i] = value
            out[i, group_slice(g), :] = value

        product(middle, coupled, g, finish)

        @pl.when(slab > 0)
        def _():
            start_sends(FOLLOWING, g)

    def interleaved(first, second, lag, between=None, after=None):
        for start in range(0, groups, WAVE):
            size = min(WAVE, groups - start)
            if between is not None and start > 0:
                between(start, size)
            for g in range(size + lag):
                if g < size:
                    first(start + g)
                if 0 <= g - lag < size:
                    second(start + g - lag)
            if after is not None and start + size < groups:
                after(start, size)

    def next_wave(start, size):
        @pl.when(slab == 0)
        def _():
            if slabs > 1:
                pl.semaphore_wait(credit_sem, 1)
            for g in range(start, start + size):
                source_copy(g, True).wait()
                start_sends(FORCING, g)

    def give_credit(name, g):
        if CREDIT[0] == name and (g - CREDIT[1]) % WAVE == 0 and g - CREDIT[1] + WAVE < groups:
            @pl.when(slab == 1)
            def _():
                pl.semaphore_signal(
                    credit_sem, inc=1, device_id={"slab": slab - 1, "space": space}, device_id_type=MESH
                )

    interleaved(forcing_task, sweep_task, LAG, next_wave)

    @pl.when(slab == 0)
    def _():
        tile_copies[1].wait()
        tile_copies[2].wait()
        turn_over(upper)
        for g in range(groups):
            wait_sends(FORCING, g)
            if slabs > 1:
                wait_sends(PREVIOUS, g)

    def wave_sent(start, size):
        for g in range(start, start + size):
            wait_sends(COUPLED, g)

    @pl.when(slab < slabs - 1)
    def _():
        interleaved(coupled_task, solution_task, LAG_BACK, after=wave_sent)

    last_wave = groups - WAVE

    @pl.when(slab > 0)
    def _():
        for g in range(groups):
            wait_sends(FORCING, g)
            wait_sends(FOLLOWING, g)

            @pl.when(slab < slabs - 1)
            def _():
                wait_sends(PREVIOUS, g)

    if slabs > 1:

        @pl.when(slab < slabs - 1)
        def _():
            for g in range(last_wave, groups):
                wait_sends(COUPLED, g)


def solution(mesh):
    slabs, spaces = mesh.shape["slab"], mesh.shape["space"]

    def shards(right_side, lower_tiles, middle_tiles, upper_tiles, columns, counts):
        _, rows, rhs, nodes = right_side.shape
        slots = columns.shape[2]
        groups = GROUPS
        width = rhs // groups
        tile_shape = lower_tiles.shape[1:]
        halo_shape = (3 * rows + 1, width, nodes)
        block_shape = (groups, rows, width, nodes)
        out = pl.pallas_call(
            functools.partial(kernel, slabs, spaces),
            out_shape=pltpu.VMEM((rows, rhs, nodes), jnp.bfloat16),
            in_specs=[pl.BlockSpec(memory_space=pltpu.SMEM)] * 2 + [pl.BlockSpec(memory_space=pltpu.MemorySpace.HBM)] * 4,
            out_specs=pl.BlockSpec(memory_space=pltpu.VMEM),
            scratch_shapes=[pltpu.VMEM(tile_shape, jnp.bfloat16)] * 3
            + [pltpu.VMEM(block_shape, jnp.bfloat16)] * 3
            + [
                pltpu.SMEM((rows * slots,), jnp.int32),
                pltpu.SemaphoreType.DMA((3,)),
                pltpu.SemaphoreType.DMA((groups,)),
                pltpu.SemaphoreType.REGULAR,
                pltpu.SemaphoreType.DMA((4, groups, 3)),
                pltpu.SemaphoreType.DMA((4, groups, 3)),
            ]
            + [pltpu.VMEM(halo_shape, jnp.bfloat16)] * (4 * groups),
            compiler_params=pltpu.CompilerParams(
                collective_id=0, has_side_effects=True, vmem_limit_bytes=60 << 20
            ),
        )(columns.transpose(2, 0, 1), counts, right_side[0], lower_tiles[0], middle_tiles[0], upper_tiles[0])
        return out[None]

    in_specs = (
        P("slab", "space", None, None),
        P("slab", "space", None, None, None),
        P("slab", "space", None, None, None),
        P("slab", "space", None, None, None),
        P("slab", "space", None),
        P("slab", "space"),
    )
    out_specs = P("slab", "space", None, None)
    return jax.shard_map(shards, mesh=mesh, in_specs=in_specs, out_specs=out_specs, check_vma=False)
```
